256 devices in a mesh: fsdp: 8 (over x, core), ctx: 32 (over y, z).
Axes of the slice: x: 4, y: 4, z: 8, core: 2. Of those that a mesh axis runs over, the one named last changes fastest.
Arguments:
- hidden: bfloat16 [8, 4096, 2304], P('fsdp', 'ctx'), may hold values from -6 to 6
- query_heads: bfloat16 [8, 4096, 2048], P('fsdp', 'ctx'), may hold values from -6 to 6
- key_heads: bfloat16 [8, 4096, 2048], P('fsdp', 'ctx'), may hold values from -6 to 6
- value_heads: bfloat16 [8, 4096, 2048], P('fsdp', 'ctx'), may hold values from -6 to 6
- out_grad: bfloat16 [8, 4096, 2048], P('fsdp', 'ctx'), may hold values from -6 to 6
- checkpoint: float32 [8, 32, 16, 128, 128], P('fsdp', 'ctx'), may hold values from -6 to 6
- gate_down: bfloat16 [2304, 128], P('fsdp'), may hold values from -0.125 to 0.125
- gate_up: bfloat16 [128, 2048], P(None, 'fsdp'), may hold values from -0.5 to 0.5
- gate_bias: float32 [2048], replicated, may hold values from -4 to 4
- decay_rate: float32 [2048], replicated, may hold values from 4.8828126e-05 to 0.05
- beta_weight: bfloat16 [2304, 16], P('fsdp'), may hold values from -0.125 to 0.125
Outputs:
- query_grad: bfloat16 [8, 4096, 2048], P('fsdp', 'ctx')
- key_grad: bfloat16 [8, 4096, 2048], P('fsdp', 'ctx')
- value_grad: bfloat16 [8, 4096, 2048], P('fsdp', 'ctx')
- hidden_grad: bfloat16 [8, 4096, 2304], P('fsdp', 'ctx')
- gate_down_grad: float32 [2304, 128], P('fsdp')
- gate_up_grad: float32 [128, 2048], P(None, 'fsdp')
- beta_weight_grad: float32 [2304, 16], P('fsdp')
- gate_bias_grad: float32 [2048], replicated
- decay_rate_grad: float32 [2048], replicated
The draws below stay inside these ranges and needn't reach their ends.
All inputs are finite; a program needn't handle non-finite values.
Results may differ from the reference program's by a relative error of at most 0.0052.
Values may be sent and summed in bfloat16 or wider, within the bound.
No kernel may reach another device: no remote copies, remote signals or barrier semaphores. Data moves between devices by JAX's collectives and lax.ppermute only.
A program may use at most 256 MiB of HBM per device.

```python
import math
import jax
import jax.numpy as jnp
from jax import lax

D = 2304
HEADS = 16
HEAD = 128
RANK = 128
CH = 128
TOK_DEV = 128
LENGTH = 4096
SEQS = 8
N_CTX = 32


def shard_levels(own_key, dims, cuts, least, largest):
    level, own = 1.0, jax.random.fold_in(own_key, 6)
    for dim, blocks in cuts:
        heights = jnp.exp(jax.random.uniform(jax.random.fold_in(own, dim), (blocks,), jnp.float32, least / len(cuts), largest / len(cuts)))
        level = level * jnp.repeat(heights, dims[dim] // blocks).reshape([-1 if axis == dim else 1 for axis in range(len(dims))])
    return level


def centred(rng, extent, spread, reach, shards=(), kind=jnp.bfloat16):
    loudness = shard_levels(rng, extent, shards, -0.22, 0.18) if shards else 1.0
    result = jax.random.normal(rng, extent, jnp.float32) * spread * loudness
    return jnp.minimum(jnp.maximum(result, -reach), reach).astype(kind)


def setup_inputs(seed: int = 0) -> dict:
    streams_of = jax.random.split(jax.random.key(seed), 12)
    return {
        "hidden": centred(streams_of[0], (SEQS, LENGTH, D), 1.0, 6.0, ((0, 8), (1, 32))),
        "query_heads": centred(streams_of[1], (SEQS, LENGTH, HEADS * HEAD), 1.0, 6.0, ((0, 8), (1, 32))),
        "key_heads": centred(streams_of[2], (SEQS, LENGTH, HEADS * HEAD), 1.0, 6.0, ((0, 8), (1, 32))),
        "value_heads": centred(streams_of[3], (SEQS, LENGTH, HEADS * HEAD), 1.0, 6.0, ((0, 8), (1, 32))),
        "out_grad": centred(streams_of[4], (SEQS, LENGTH, HEADS * HEAD), 1.0, 6.0, ((0, 8), (1, 32))),
        "checkpoint": centred(streams_of[5], (SEQS, N_CTX, HEADS, HEAD, HEAD), 1.0, 6.0, ((0, 8), (1, 32)), jnp.float32),
        "gate_down": centred(streams_of[6], (D, RANK), D ** -0.5, 0.125, ((0, 8),)),
        "gate_up": centred(streams_of[7], (RANK, HEADS * HEAD), RANK ** -0.5, 0.5, ((1, 8),)),
        "gate_bias": centred(streams_of[8], (HEADS * HEAD,), 1.0, 4.0, (), jnp.float32),
        "decay_rate": jnp.clip(jnp.exp(jax.random.uniform(streams_of[9], (HEADS * HEAD,), jnp.float32, math.log(4.882812572759576e-05), math.log(0.05))), 4.882812572759576e-05, 0.05),
        "beta_weight": centred(streams_of[10], (D, HEADS), D ** -0.5, 0.125, ((0, 8),)),
    }


PRECISE = lax.Precision.HIGHEST
EPSILON = 1e-06

def unit_rows(matrix):
    return matrix * lax.rsqrt(lax.optimization_barrier(jnp.sum(matrix * matrix, axis=-1, keepdims=True)) + EPSILON)

def to_spans(values):
    tok_rows = values.shape[0]
    return values.reshape((tok_rows // CH, CH) + values.shape[1:]).swapaxes(1, 2)

def tri_masks():
    row_index = lax.broadcasted_iota(jnp.int32, (CH, CH), 0)
    col_index = lax.broadcasted_iota(jnp.int32, (CH, CH), 1)
    return ((row_index > col_index).astype(jnp.float32), (row_index >= col_index).astype(jnp.float32))

def span_terms(k_span, g_span, b_span):
    cumulative = jnp.cumsum(g_span, axis=1)
    key_plus = k_span * jnp.exp(cumulative)
    key_minus = k_span * jnp.exp(-cumulative)
    key_end = k_span * jnp.exp(cumulative[:, -1:, :] - cumulative)
    strict, _ = tri_masks()
    mixing = jnp.einsum('htc,hsc->hts', key_plus, key_minus, precision=PRECISE) * strict * b_span[:, :, None]
    system = mixing + jnp.eye(CH, dtype=jnp.float32)
    return (cumulative, key_plus, key_minus, key_end, system)

def block_forward(start_state, queries, keys_in, values_in, decay_heads, beta_gate):
    q_all = to_spans(unit_rows(queries))
    k_all = to_spans(unit_rows(keys_in))
    v_all = to_spans(values_in)
    g_all = to_spans(decay_heads)
    b_all = to_spans(beta_gate)
    _, inclusive = tri_masks()

    def advance(carried, pieces):
        q_span, k_span, v_span, g_span, b_span = pieces
        cumulative, key_plus, key_minus, key_end, system = span_terms(k_span, g_span, b_span)
        query_plus = q_span * jnp.exp(cumulative)
        target = b_span[:, :, None] * (v_span - jnp.einsum('htc,hcd->htd', key_plus, carried, precision=PRECISE))
        updates = jax.scipy.linalg.solve_triangular(system, target, lower=True, unit_diagonal=True)
        scores = jnp.einsum('htc,hsc->hts', query_plus, key_minus, precision=PRECISE) * inclusive
        outputs = jnp.einsum('htc,hcd->htd', query_plus, carried, precision=PRECISE) + jnp.einsum('hts,hsd->htd', scores, updates, precision=PRECISE)
        renewed = jnp.exp(cumulative[:, -1, :])[:, :, None] * carried + jnp.einsum('hsc,hsd->hcd', key_end, updates, precision=PRECISE)
        return (renewed, outputs)
    end_state, outputs = lax.scan(advance, start_state, (q_all, k_all, v_all, g_all, b_all))
    return (outputs.swapaxes(1, 2).reshape(queries.shape), end_state)

def gate_forward(hidden_rows, down_full, up_full, gate_bias, decay_rate, beta_full):
    low_rank = jnp.dot(hidden_rows.astype(jnp.float32), down_full.astype(jnp.float32), preferred_element_type=jnp.float32).astype(jnp.bfloat16)
    gate_input = jnp.dot(low_rank.astype(jnp.float32), up_full.astype(jnp.float32), preferred_element_type=jnp.float32) + gate_bias
    log_decay = -decay_rate * jax.nn.softplus(gate_input)
    beta_gate = jax.nn.sigmoid(jnp.dot(hidden_rows.astype(jnp.float32), beta_full.astype(jnp.float32), preferred_element_type=jnp.float32))
    return (low_rank, gate_input, log_decay, beta_gate)

def contract_rows(left, right):
    return lax.dot_general(left.astype(jnp.float32), right.astype(jnp.float32), (((0,), (0,)), ((), ())), preferred_element_type=jnp.float32)

def contract_cols(left, right):
    return lax.dot_general(left.astype(jnp.float32), right.astype(jnp.float32), (((1,), (1,)), ((), ())), preferred_element_type=jnp.float32)

def gate_backward(hidden_rows, low_rank, gate_input, beta_gate, decay_cot, beta_cot, down_full, up_full, decay_rate, beta_full):
    input_grad = decay_cot * -decay_rate * jax.nn.sigmoid(gate_input)
    input_half = input_grad.astype(jnp.bfloat16)
    rate_term = -lax.optimization_barrier(jnp.sum(decay_cot * jax.nn.softplus(gate_input), axis=0))
    bias_term = lax.optimization_barrier(jnp.sum(input_grad, axis=0))
    up_term = contract_rows(low_rank, input_half)
    low_grad = contract_cols(input_half, up_full).astype(jnp.bfloat16)
    score_grad = (beta_cot * beta_gate * (1.0 - beta_gate)).astype(jnp.bfloat16)
    down_term = contract_rows(hidden_rows, low_grad)
    beta_term = contract_rows(hidden_rows, score_grad)
    hidden_grad = (contract_cols(low_grad, down_full) + contract_cols(score_grad, beta_full)).astype(jnp.bfloat16)
    return (hidden_grad, down_term, up_term, beta_term, bias_term, rate_term)

def reference(hidden, query_heads, key_heads, value_heads, out_grad, checkpoint, gate_down, gate_up, gate_bias, decay_rate, beta_weight):
    seq_count, seq_length, model_width = hidden.shape
    count_heads, size_head = (checkpoint.shape[2], checkpoint.shape[3])
    hidden_rows = hidden.reshape(seq_count * seq_length, model_width)
    low_rank, gate_input, log_decay, beta_gate = gate_forward(hidden_rows, gate_down, gate_up, gate_bias, decay_rate, beta_weight)

    def blocked(values, trailing):
        return values.reshape((seq_count, N_CTX, TOK_DEV) + trailing).swapaxes(0, 1)
    full_heads = (count_heads, size_head)

    def one_block(start_state, queries, keys_in, values_in, decay_block, beta_block, grad_block, end_grad):
        _, pullback = jax.vjp(block_forward, start_state, queries.astype(jnp.float32), keys_in.astype(jnp.float32), values_in.astype(jnp.float32), decay_block, beta_block)
        start_grad, q_grad, k_grad, v_grad, d_grad, b_grad = pullback((grad_block.astype(jnp.float32), end_grad))
        return (start_grad, q_grad.astype(jnp.bfloat16), k_grad.astype(jnp.bfloat16), v_grad.astype(jnp.bfloat16), d_grad, b_grad)
    batched = jax.vmap(one_block)

    def backward_step(end_grad, pieces):
        results = batched(pieces[0], pieces[1], pieces[2], pieces[3], pieces[4], pieces[5], pieces[6], end_grad)
        return (results[0], results[1:])
    pieces = (checkpoint.swapaxes(0, 1), blocked(query_heads, full_heads), blocked(key_heads, full_heads), blocked(value_heads, full_heads), blocked(log_decay, full_heads), blocked(beta_gate, (count_heads,)), blocked(out_grad, full_heads))
    zero_grad = jnp.zeros((seq_count, count_heads, size_head, size_head), jnp.float32)
    _, stacked = lax.scan(backward_step, zero_grad, pieces, reverse=True)

    def unblock(values):
        return values.swapaxes(0, 1).reshape(seq_count, seq_length, -1)
    query_grad = unblock(stacked[0])
    key_grad = unblock(stacked[1])
    value_grad = unblock(stacked[2])
    decay_cot = unblock(stacked[3]).reshape(seq_count * seq_length, -1)
    beta_cot = unblock(stacked[4]).reshape(seq_count * seq_length, -1)
    hidden_grad, down_term, up_term, beta_term, bias_term, rate_term = gate_backward(hidden_rows, low_rank, gate_input, beta_gate, decay_cot, beta_cot, gate_down, gate_up, decay_rate, beta_weight)
    return (query_grad, key_grad, value_grad, hidden_grad.reshape(seq_count, seq_length, model_width), down_term, up_term, beta_term, bias_term, rate_term)
```

```python
import functools

import jax
import jax.numpy as jnp
from jax import lax
from jax.experimental import pallas as pl
from jax.experimental.pallas import tpu as pltpu
from jax.sharding import Mesh, PartitionSpec as P

EPSILON = 1e-06
BF = jnp.bfloat16
F32 = jnp.float32
N = 128
HB = 4
FIRST_HB = 8
INTERPRET = False


def split(x):
    hi = x.astype(BF)
    return [hi, (x - hi.astype(F32)).astype(BF)]


def split3(x):
    hi = x.astype(BF)
    rest = x - hi.astype(F32)
    mid = rest.astype(BF)
    return [hi, mid, (rest - mid.astype(F32)).astype(BF)]


def dot(a, b, ca=1, cb=0):
    return lax.dot_general(a, b, (((ca,), (cb,)), ((), ())), preferred_element_type=F32)


def mm(a, b, ca=1, cb=0):
    if len(a) > 1 and len(b) > 1:
        both = jnp.concatenate(b, axis=1 - cb)
        both = dot(jnp.concatenate(a, axis=ca), jnp.concatenate([both, both], axis=cb), ca, cb)
        half = both.shape[1] // 2
        return both[:, :half] + both[:, half:]
    if len(a) > 1:
        return dot(jnp.concatenate(a, axis=ca), jnp.concatenate([b[0], b[0]], axis=cb), ca, cb)
    return sum(dot(a[0], part, ca, cb) for part in b)


def iotas():
    return lax.broadcasted_iota(jnp.int32, (N, N), 0), lax.broadcasted_iota(jnp.int32, (N, N), 1)


def ones_where(cond):
    return jnp.where(cond, 1.0, 0.0).astype(BF)


def softplus(x):
    return jnp.maximum(x, 0.0) + jnp.log1p(jnp.exp(-jnp.abs(x)))


def unit(x):
    scale = lax.rsqrt(jnp.sum(x * x, axis=-1, keepdims=True) + EPSILON)
    return x * scale, scale


def column(values, index):
    lane = lax.broadcasted_iota(jnp.int32, values.shape, 1)
    return jnp.sum(jnp.where(lane == index, values, 0.0), axis=1, keepdims=True)


def inverses(stricts, row, col):
    near = (row >> 3) == (col >> 3)
    gather = ones_where(near)
    lane = lax.broadcasted_iota(jnp.int32, (8, N), 1) & 7
    sub = lax.broadcasted_iota(jnp.int32, (8, N), 0)
    invs = []
    for strict in stricts:
        block = jnp.where(near, strict, 0.0)
        block = sum(block[8 * i:8 * i + 8] for i in range(N // 8))
        picked = split3(jnp.concatenate([jnp.where(lane == k, block, 0.0) for k in range(8)], axis=0))
        spread = sum(dot(part, gather) for part in picked)
        inv = jnp.where(lane == sub, 1.0, 0.0)
        for k in range(7):
            inv = inv - spread[8 * k:8 * k + 8] * inv[k:k + 1, :]
        invs.append(jnp.where(near, jnp.concatenate([inv] * (N // 8), axis=0), 0.0))
    for bit in range(3, 7):
        pick = ((row >> (bit + 1)) == (col >> (bit + 1))) & ((row >> bit) != (col >> bit))
        parts = [split(inv) for inv in invs]
        offs = [split(jnp.where(pick, strict, 0.0)) for strict in stricts]
        offs = [split(mm(part, off)) for part, off in zip(parts, offs)]
        invs = [inv - mm(off, part) for inv, off, part in zip(invs, offs, parts)]
    return invs


def head_columns(count):
    return [slice(i * N, (i + 1) * N) for i in range(count)]


def first_kernel(low_ref, up_ref, bias_ref, rate_ref, beta_ref, q_ref, k_ref, g_ref,
                 send_ref, inv_ref, mix_ref, sco_ref, cum_ref):
    count = inv_ref.shape[0]
    base = pl.program_id(0) * count
    row, col = iotas()
    tri = ones_where(row >= col)
    cols = head_columns(count)
    each = lambda f: [f(i) for i in range(count)]
    gate = each(lambda i: dot(low_ref[...], up_ref[i]) + bias_ref[:, cols[i]])
    decay = each(lambda i: split3(-rate_ref[:, cols[i]] * softplus(gate[i])))
    cum = each(lambda i: sum(dot(tri, piece) for piece in decay[i]))
    for i in range(count):
        cum_ref[i] = cum[i]
    last = each(lambda i: cum[i][N - 1:N, :])
    qn = each(lambda i: unit(q_ref[:, cols[i]].astype(F32))[0])
    kn = each(lambda i: unit(k_ref[:, cols[i]].astype(F32))[0])
    scale = each(lambda i: jnp.exp(cum[i]))
    kp = each(lambda i: kn[i] * scale[i])
    qp = each(lambda i: qn[i] * scale[i])
    km = each(lambda i: split(kn[i] * jnp.exp(-cum[i])))
    beta = each(lambda i: column(beta_ref[...], base + i))
    mix = each(lambda i: jnp.where(row > col, mm(split(kp[i]), km[i], 1, 1), 0.0))
    sco = each(lambda i: jnp.where(row >= col, mm(split(qp[i]), km[i], 1, 1), 0.0))
    for i in range(count):
        mix_ref[i] = mix[i]
        sco_ref[i] = sco[i]
    inv = inverses(each(lambda i: mix[i] * beta[i]), row, col)
    for i in range(count):
        inv_ref[i] = inv[i]
    z = each(lambda i: split(mm(split(inv[i]), split(kp[i] * beta[i]))))
    seen = each(lambda i: split(qp[i] - mm(split(sco[i]), z[i])))
    local = each(lambda i: mm(seen[i], [g_ref[:, cols[i]]], 0, 0))
    ke = each(lambda i: split(kn[i] * jnp.exp(last[i] - cum[i])))
    moving = each(lambda i: jnp.where(row == col, jnp.exp(last[i]), 0.0) - mm(z[i], ke[i], 0, 0))
    for i in range(count):
        send_ref[i, 0:N, :] = moving[i].astype(BF)
        send_ref[i, N:2 * N, :] = local[i].astype(BF)


def chain_kernel(got_ref, all_ref, tot_ref):
    blocks, heads = got_ref.shape[0], got_ref.shape[1]
    each = lambda f: [f(h) for h in range(heads)]
    both = each(lambda h: jnp.concatenate(
        [got_ref[blocks - 1, h, 0:N, :], got_ref[blocks - 1, h, N:2 * N, :]], axis=1).astype(F32))
    for j in range(blocks - 1, -1, -1):
        if j < blocks - 1:
            both = each(lambda h: mm([got_ref[j, h, 0:N, :]], split(both[h])))
            both = each(lambda h: jnp.concatenate(
                [both[h][:, :N], both[h][:, N:] + got_ref[j, h, N:2 * N, :].astype(F32)], axis=1))
        for h in range(heads):
            all_ref[j, h] = both[h]
    for h in range(heads):
        tot_ref[h] = both[h].astype(BF)


def apply_kernel(all_ref, *refs):
    *later, end_ref = refs
    blocks, heads = all_ref.shape[0], all_ref.shape[1]
    each = lambda f: [f(h) for h in range(heads)]
    carry = each(lambda h: jnp.zeros((N, N), F32))
    for ref in later:
        carry = each(lambda h: mm([ref[h, :, 0:N]], split(carry[h])) + ref[h, :, N:2 * N].astype(F32))
    for h in range(heads):
        end_ref[blocks - 1, h] = carry[h].astype(BF)
    carry = each(lambda h: split(carry[h]))
    for j in range(blocks - 1):
        for h in range(heads):
            end_ref[j, h] = (mm(split(all_ref[j + 1, h, :, :N]), carry[h])
                             + all_ref[j + 1, h, :, N:]).astype(BF)


def middle_kernel(beta_ref, q_ref, k_ref, v_ref, g_ref, start_ref, inv_ref, sco_ref, cum_ref,
                  qg_ref, rest_ref, upd_ref, y_ref, kms_ref, term_ref):
    count = inv_ref.shape[0]
    base = pl.program_id(0) * count
    row, col = iotas()
    cols = head_columns(count)
    each = lambda f: [f(i) for i in range(count)]
    cum = each(lambda i: cum_ref[i])
    q = each(lambda i: unit(q_ref[:, cols[i]].astype(F32)))
    kn = each(lambda i: unit(k_ref[:, cols[i]].astype(F32))[0])
    plus = each(lambda i: jnp.exp(cum[i]))
    qp = each(lambda i: q[i][0] * plus[i])
    km = each(lambda i: split(kn[i] * jnp.exp(-cum[i])))
    beta = each(lambda i: column(beta_ref[...], base + i))
    grad = each(lambda i: [g_ref[:, cols[i]]])
    start = each(lambda i: split(start_ref[i]))
    inv = each(lambda i: split(inv_ref[i]))
    rest = each(lambda i: v_ref[:, cols[i]].astype(F32) - mm(split(kn[i] * plus[i]), start[i]))
    upd = each(lambda i: mm(inv[i], split(rest[i] * beta[i])))
    y = each(lambda i: mm(inv[i], split(mm(split(sco_ref[i]), grad[i], 0, 0)), 0, 0))
    upd_s = each(lambda i: split(upd[i]))
    sco_cot = each(lambda i: split(jnp.where(row >= col, mm(grad[i], upd_s[i], 1, 1), 0.0)))
    qp_cot = each(lambda i: mm(grad[i], start[i], 1, 1) + mm(sco_cot[i], km[i]))
    kms = each(lambda i: mm(sco_cot[i], split(qp[i]), 0, 0))
    qn_cot = each(lambda i: qp_cot[i] * plus[i])
    for i in range(count):
        rest_ref[i] = rest[i]
        upd_ref[i] = upd[i]
        y_ref[i] = y[i]
        kms_ref[i] = kms[i]
        term_ref[i] = qp_cot[i] * qp[i]
        qg_ref[:, i * N:(i + 1) * N] = (q[i][1] * (
            qn_cot[i] - q[i][0] * jnp.sum(qn_cot[i] * q[i][0], axis=1, keepdims=True))).astype(BF)


def second_kernel(low_ref, up_ref, bias_ref, rate_ref, beta_ref, k_ref, start_ref, end_ref,
                  inv_ref, mix_ref, cum_ref, rest_ref, upd_ref, y_ref, kms_ref, term_ref,
                  kg_ref, vg_ref, half_ref, vec_ref, lowg_ref, score_ref, low_acc, score_acc):
    count = inv_ref.shape[0]
    step = pl.program_id(0)
    base = step * count
    row, col = iotas()
    upper = ones_where(row <= col)
    ones = jnp.ones((8, N), BF)

    @pl.when(step == 0)
    def _():
        low_acc[...] = jnp.zeros_like(low_acc)
        score_acc[...] = jnp.zeros_like(score_acc)

    cols = head_columns(count)
    each = lambda f: [f(i) for i in range(count)]
    cum = each(lambda i: cum_ref[i])
    last = each(lambda i: cum[i][N - 1:N, :])
    k = each(lambda i: unit(k_ref[:, cols[i]].astype(F32)))
    plus = each(lambda i: jnp.exp(cum[i]))
    minus = each(lambda i: jnp.exp(-cum[i]))
    ending = each(lambda i: jnp.exp(last[i] - cum[i]))
    kp = each(lambda i: k[i][0] * plus[i])
    km = each(lambda i: k[i][0] * minus[i])
    ke = each(lambda i: k[i][0] * ending[i])
    beta = each(lambda i: column(beta_ref[...], base + i))
    end = each(lambda i: [end_ref[i]])
    upd = each(lambda i: split(upd_ref[i]))
    y = each(lambda i: y_ref[i] + mm(split(inv_ref[i]), split(mm(split(ke[i]), end[i])), 0, 0))
    rest_cot = each(lambda i: y[i] * beta[i])
    for i in range(count):
        vg_ref[:, cols[i]] = rest_cot[i].astype(BF)
    outer = each(lambda i: jnp.where(row > col, mm(split(y[i]), upd[i], 1, 1), 0.0))
    beta_cot = each(lambda i: jnp.sum(y[i] * rest_ref[i] - outer[i] * mix_ref[i], axis=1, keepdims=True))
    mix_cot = each(lambda i: split(-outer[i] * beta[i]))
    kp_cot = each(lambda i: mm(mix_cot[i], split(km[i]))
                  - mm(split(rest_cot[i]), split(start_ref[i]), 1, 1))
    km_cot = each(lambda i: mm(mix_cot[i], split(kp[i]), 0, 0) + kms_ref[i])
    ke_cot = each(lambda i: mm(upd[i], end[i], 1, 1))
    last_cot = each(lambda i: jnp.sum(ke_cot[i] * ke[i], axis=0, keepdims=True) + jnp.exp(last[i]) * sum(
        dot(ones, piece, 1, 1) for piece in split3(start_ref[i] * end_ref[i].astype(F32)))[0:1, :])
    cum_cot = each(lambda i: split3(
        term_ref[i] + kp_cot[i] * kp[i] - km_cot[i] * km[i] - ke_cot[i] * ke[i]))
    decay_cot = each(lambda i: sum(dot(upper, piece) for piece in cum_cot[i]) + last_cot[i])
    kn_cot = each(lambda i: kp_cot[i] * plus[i] + km_cot[i] * minus[i] + ke_cot[i] * ending[i])
    for i in range(count):
        kg_ref[:, cols[i]] = (k[i][1] * (
            kn_cot[i] - k[i][0] * jnp.sum(kn_cot[i] * k[i][0], axis=1, keepdims=True))).astype(BF)
    up = each(lambda i: up_ref[i])
    gate = each(lambda i: dot(low_ref[...], up[i]) + bias_ref[:, cols[i]])
    input_grad = each(lambda i: decay_cot[i] * -rate_ref[:, cols[i]] * jax.nn.sigmoid(gate[i]))
    half = each(lambda i: input_grad[i].astype(BF))
    for i in range(count):
        half_ref[i] = half[i]
        vec_ref[i] = jnp.concatenate([
            jnp.sum(input_grad[i], axis=0, keepdims=True),
            -jnp.sum(decay_cot[i] * softplus(gate[i]), axis=0, keepdims=True)], axis=0)
    low_acc[...] += sum(each(lambda i: dot(half[i], up[i], 1, 1)))
    score_acc[...] += sum(each(lambda i: jnp.where(
        col == base + i, beta_cot[i] * beta[i] * (1.0 - beta[i]), 0.0)))

    @pl.when(step == pl.num_programs(0) - 1)
    def _():
        lowg_ref[...] = low_acc[...].astype(BF)
        score_ref[...] = score_acc[...].T[0:score_ref.shape[0], :].astype(BF)


def weights_kernel(hid_ref, got_ref, out_ref, *, heads, rows):
    seqs = got_ref.shape[0]
    low_at = heads * N
    score_at = low_at + N
    down = jnp.zeros((rows, N), F32)
    beta = jnp.zeros((16, rows), F32)
    ups = [jnp.zeros((N, N), F32) for _ in range(heads)]
    vec = jnp.zeros((got_ref.shape[1] - score_at - 16, N), F32)
    for s in range(seqs):
        hid = hid_ref[s, 0:rows, :]
        rank = hid_ref[s, rows:rows + N, :]
        down = down + dot(hid, got_ref[s, low_at:low_at + N, :])
        beta = beta + dot(got_ref[s, score_at:score_at + 16, :], hid, 1, 1)
        for h in range(heads):
            ups[h] = ups[h] + dot(rank, got_ref[s, h * N:(h + 1) * N, :], 0, 0)
        vec = vec + got_ref[s, score_at + 16:, :].astype(F32)
    half = vec.shape[0] // 2
    at = 0
    for up in ups:
        out_ref[at:at + N, :] = up
        at += N
    out_ref[at:at + rows, :] = down
    at += rows
    out_ref[at:at + half, :] = vec[:half] + vec[half:]
    at += half
    for piece in range(0, rows, N):
        width = min(N, rows - piece)
        if width < N:
            out_ref[at:at + 16, :] = jnp.zeros((16, N), F32)
        out_ref[at:at + 16, 0:width] = beta[:, piece:piece + width]
        at += 16
    out_ref[at:, :] = jnp.zeros((out_ref.shape[0] - at, N), F32)


def call(kernel, name, **kw):
    return pl.pallas_call(kernel, interpret=INTERPRET, name=name,
                          compiler_params=pltpu.CompilerParams(vmem_limit_bytes=56 << 20), **kw)


def shape(dims, dtype):
    return jax.ShapeDtypeStruct(dims, dtype)


def on_device(nf, ny, nz, hidden, query_heads, key_heads, value_heads, out_grad, checkpoint,
              gate_down, gate_up, gate_bias, decay_rate, beta_weight):
    tok, width = hidden.shape[1], hidden.shape[2]
    heads = checkpoint.shape[2]
    inner = heads * N
    rows = width // nf
    own = heads // nf
    group = heads // nz
    hidden_rows = hidden.reshape(tok, width)

    beta_rows = rows * heads // N
    up_rows = own * N
    mine = jnp.concatenate([
        gate_up.reshape(N, own, N).swapaxes(0, 1).reshape(up_rows, N),
        gate_down,
        beta_weight.reshape(beta_rows, N)], axis=0)
    mine = jnp.pad(mine, ((0, -mine.shape[0] % 16), (0, 0)))
    got = lax.all_to_all(jnp.broadcast_to(mine[None], (nf,) + mine.shape), "fsdp", 0, 0, tiled=True)
    ups = got[:, :up_rows, :].reshape(heads, N, N)
    down_full = got[:, up_rows:up_rows + rows, :].reshape(width, N)
    beta_full = got[:, up_rows + rows:up_rows + rows + beta_rows, :].reshape(width, heads)

    low_rank = jnp.dot(hidden_rows, down_full, preferred_element_type=F32).astype(BF)
    beta_gate = jax.nn.sigmoid(jnp.dot(hidden_rows, beta_full, preferred_element_type=F32))
    bias = gate_bias.reshape(1, inner)
    rate = decay_rate.reshape(1, inner)
    q, k, v, g = (x.reshape(tok, inner) for x in (query_heads, key_heads, value_heads, out_grad))
    start = checkpoint.reshape(heads, N, N)

    whole = lambda dims: pl.BlockSpec(dims, lambda i: (0,) * len(dims))
    row_spec = lambda hb: pl.BlockSpec((1, hb * N), lambda i: (0, i))
    tok_spec = lambda hb: pl.BlockSpec((N, hb * N), lambda i: (0, i))
    mat_spec = lambda hb: pl.BlockSpec((hb, N, N), lambda i: (i, 0, 0))
    gate_specs = lambda hb: [
        whole((tok, N)), mat_spec(hb), row_spec(hb), row_spec(hb), whole((tok, heads))]
    gate_args = (low_rank, ups, bias, rate, beta_gate)
    mat = shape((heads, N, N), F32)
    cost = pl.CostEstimate(flops=4 * 10**9, bytes_accessed=12 << 20, transcendentals=0)

    hb = FIRST_HB
    send, inv, mix, sco, cum = call(
        first_kernel, "first",
        grid=(heads // hb,),
        in_specs=gate_specs(hb) + [tok_spec(hb)] * 3,
        out_specs=[pl.BlockSpec((hb, 2 * N, N), lambda i: (i, 0, 0))] + [mat_spec(hb)] * 4,
        out_shape=[shape((heads, 2 * N, N), BF)] + [mat] * 4,
    )(*gate_args, q, k, g)

    spread = lax.all_to_all(send, "z", 0, 0, tiled=True).reshape(nz, group, 2 * N, N)

    hb = HB
    q_grad, rest, upd, y, kms, term = call(
        middle_kernel, "middle",
        grid=(heads // hb,),
        in_specs=[whole((tok, heads))] + [tok_spec(hb)] * 4 + [mat_spec(hb)] * 4,
        out_specs=[tok_spec(hb)] + [mat_spec(hb)] * 5,
        out_shape=[shape((tok, inner), BF)] + [mat] * 5,
        cost_estimate=cost,
    )(beta_gate, q, k, v, g, start, inv, sco, cum)

    every, total = call(
        chain_kernel, "chain",
        out_shape=[shape((nz, group, N, 2 * N), F32), shape((group, N, 2 * N), BF)],
    )(spread)
    later = [lax.ppermute(total, "y", [(y + d, y) for y in range(ny - d)])
             for d in range(ny - 1, 0, -1)]
    end = call(apply_kernel, "apply", out_shape=shape((nz, group, N, N), BF))(every, *later)
    end = lax.all_to_all(end.reshape(heads, N, N), "z", 0, 0, tiled=True)

    early = jnp.concatenate([
        hidden_rows.T.reshape(nf, rows, tok),
        jnp.broadcast_to(low_rank[None], (nf, tok, N))], axis=1)
    end, early = lax.optimization_barrier((end, early))
    early = lax.all_to_all(early, "fsdp", 0, 0, tiled=True)

    k_grad, v_grad, half, vec, low_grad, score = call(
        second_kernel, "second",
        grid=(heads // hb,),
        in_specs=gate_specs(hb) + [tok_spec(hb)] + [mat_spec(hb)] * 10,
        out_specs=[tok_spec(hb)] * 2 + [
            mat_spec(hb), pl.BlockSpec((hb, 2, N), lambda i: (i, 0, 0)),
            whole((N, N)), whole((heads, N))],
        out_shape=[shape((tok, inner), BF)] * 2 + [
            shape((heads, N, N), BF), shape((heads, 2, N), F32),
            shape((N, N), BF), shape((heads, N), BF)],
        scratch_shapes=[pltpu.VMEM((N, N), F32)] * 2,
        cost_estimate=cost,
    )(*gate_args, k, start, end, inv, mix, cum, rest, upd, y, kms, term)

    vec = vec.reshape(2 * heads, N)
    vec_hi = vec.astype(BF)
    vec_lo = (vec - vec_hi.astype(F32)).astype(BF)
    common = jnp.concatenate([low_grad, score, vec_hi, vec_lo], axis=0)
    terms = jnp.concatenate([
        half.reshape(nf, own * N, N),
        jnp.broadcast_to(common[None], (nf,) + common.shape)], axis=1)
    terms = lax.all_to_all(terms, "fsdp", 0, 0, tiled=True)
    beta_out = 16 * -(-rows // N)
    used = own * N + rows + 2 * heads + beta_out
    parts = ny * nz
    chunk = 8 * -(-used // (8 * parts))
    sums = call(
        functools.partial(weights_kernel, heads=own, rows=rows), "weights",
        out_shape=shape((parts * chunk, N), F32),
    )(early, terms)
    sums = lax.all_to_all(sums.reshape(parts, chunk, N), ("y", "z"), 0, 0, tiled=True)
    sums = jnp.broadcast_to(jnp.sum(sums, axis=0)[None], (parts, chunk, N))
    sums = lax.all_to_all(sums, ("y", "z"), 0, 0, tiled=True).reshape(parts * chunk, N)
    at = own * N
    up_grad = sums[:at].reshape(own, N, N).swapaxes(0, 1).reshape(N, own * N)
    down_grad = sums[at:at + rows]
    at += rows
    vectors = sums[at:at + 2 * heads].reshape(heads, 2, N).swapaxes(0, 1).reshape(2, inner)
    at += 2 * heads
    beta_grad = sums[at:at + beta_out].reshape(-1, 16, N).swapaxes(0, 1).reshape(16, -1)
    beta_grad = beta_grad[:, :rows].T

    hidden_grad = (
        lax.dot_general(low_grad, down_full, (((1,), (1,)), ((), ())), preferred_element_type=F32)
        + lax.dot_general(score, beta_full, (((0,), (1,)), ((), ())), preferred_element_type=F32)
    ).astype(BF)

    return (q_grad[None], k_grad[None], v_grad[None], hidden_grad[None],
            down_grad, up_grad, beta_grad, vectors[0], vectors[1])


def grid_of(size):
    ny = 1
    while ny * ny * 4 <= size:
        ny *= 2
    return ny, size // ny


def solution(mesh):
    nf, size = mesh.shape["fsdp"], mesh.shape["ctx"]
    ny, nz = grid_of(size)
    fine = Mesh(mesh.devices.reshape(nf, ny, nz), ("fsdp", "y", "z"))
    ctx = ("y", "z")
    tokens = P("fsdp", ctx, None)
    return jax.shard_map(
        functools.partial(on_device, nf, ny, nz),
        mesh=fine,
        in_specs=(tokens,) * 5 + (
            P("fsdp", ctx, None, None, None), P("fsdp", None), P(None, "fsdp"), P(), P(),
            P("fsdp", None)),
        out_specs=(tokens,) * 4 + (
            P("fsdp", None), P(None, "fsdp"), P("fsdp", None), P(), P()),
        check_vma=False,
    )
```

```python
import functools

import jax
import jax.numpy as jnp
from jax import lax
from jax.experimental import pallas as pl
from jax.experimental.pallas import tpu as pltpu
from jax.sharding import Mesh, PartitionSpec as P

EPSILON = 1e-06
BF = jnp.bfloat16
F32 = jnp.float32
N = 128
HB = 4
FIRST_HB = 8
LINK = jnp.bfloat16
RUN = 4
MIB = 28
INTERPRET = False


def split(x):
    hi = x.astype(BF)
    return [hi, (x - hi.astype(F32)).astype(BF)]


def split3(x):
    hi = x.astype(BF)
    rest = x - hi.astype(F32)
    mid = rest.astype(BF)
    return [hi, mid, (rest - mid.astype(F32)).astype(BF)]


def dot(a, b, ca=1, cb=0):
    return lax.dot_general(a, b, (((ca,), (cb,)), ((), ())), preferred_element_type=F32)


def mm(a, b, ca=1, cb=0):
    if len(a) > 1 and len(b) > 1:
        both = jnp.concatenate(b, axis=1 - cb)
        both = dot(jnp.concatenate(a, axis=ca), jnp.concatenate([both, both], axis=cb), ca, cb)
        half = both.shape[1] // 2
        return both[:, :half] + both[:, half:]
    if len(a) > 1:
        return dot(jnp.concatenate(a, axis=ca), jnp.concatenate([b[0], b[0]], axis=cb), ca, cb)
    return sum(dot(a[0], part, ca, cb) for part in b)


def iotas():
    return lax.broadcasted_iota(jnp.int32, (N, N), 0), lax.broadcasted_iota(jnp.int32, (N, N), 1)


def ones_where(cond):
    return jnp.where(cond, 1.0, 0.0).astype(BF)


def softplus(x):
    return jnp.maximum(x, 0.0) + jnp.log1p(jnp.exp(-jnp.abs(x)))


def unit(x):
    scale = lax.rsqrt(jnp.sum(x * x, axis=-1, keepdims=True) + EPSILON)
    return x * scale, scale


def column(values, index):
    lane = lax.broadcasted_iota(jnp.int32, values.shape, 1)
    return jnp.sum(jnp.where(lane == index, values, 0.0), axis=1, keepdims=True)


def inverses(stricts, row, col):
    near = (row >> 3) == (col >> 3)
    gather = ones_where(near)
    lane = lax.broadcasted_iota(jnp.int32, (8, N), 1) & 7
    sub = lax.broadcasted_iota(jnp.int32, (8, N), 0)
    invs = []
    for strict in stricts:
        block = jnp.where(near, strict, 0.0)
        block = sum(block[8 * i:8 * i + 8] for i in range(N // 8))
        picked = split3(jnp.concatenate([jnp.where(lane == k, block, 0.0) for k in range(8)], axis=0))
        spread = sum(dot(part, gather) for part in picked)
        inv = jnp.where(lane == sub, 1.0, 0.0)
        for k in range(7):
            inv = inv - spread[8 * k:8 * k + 8] * inv[k:k + 1, :]
        invs.append(jnp.where(near, jnp.concatenate([inv] * (N // 8), axis=0), 0.0))
    for bit in range(3, 7):
        pick = ((row >> (bit + 1)) == (col >> (bit + 1))) & ((row >> bit) != (col >> bit))
        parts = [split(inv) for inv in invs]
        offs = [split(jnp.where(pick, strict, 0.0)) for strict in stricts]
        offs = [split(mm(part, off)) for part, off in zip(parts, offs)]
        invs = [inv - mm(off, part) for inv, off, part in zip(invs, offs, parts)]
    return invs


def head_columns(count):
    return [slice(i * N, (i + 1) * N) for i in range(count)]


def pad_to_square(x):
    if x.shape[0] < N:
        x = jnp.concatenate([x, jnp.zeros((N - x.shape[0], x.shape[1]), x.dtype)], axis=0)
    if x.shape[1] < N:
        x = jnp.concatenate([x, jnp.zeros((N, N - x.shape[1]), x.dtype)], axis=1)
    return x


def widen(x):
    if x.shape[1] == N:
        return x
    return jnp.concatenate([x, jnp.zeros((x.shape[0], N - x.shape[1]), x.dtype)], axis=1)


def pack_kernel(up_ref, down_ref, beta_ref, out_ref):
    rows = beta_ref.shape[1]
    parts = [up_ref[:, a:a + N] for a in range(0, up_ref.shape[1], N)] + [down_ref[...]]
    parts += [widen(beta_ref[:, a:min(a + N, rows)]) for a in range(0, rows, N)]
    mine = jnp.concatenate(parts, axis=0)
    for r in range(out_ref.shape[0]):
        out_ref[r] = mine


def arrange_kernel(core_ref, ours_ref, theirs_ref, hidden_ref, turned_ref,
                   up_ref, down_ref, betas_ref, low_ref, gate_ref, *, rows):
    pairs = ours_ref.shape[0]
    heads = gate_ref.shape[1]
    own = up_ref.shape[0] // (2 * pairs)
    core = core_ref[0]
    logits = jnp.zeros((heads, N), F32)
    for ref, place in ((ours_ref, core), (theirs_ref, 1 - core)):
        for x in range(pairs):
            owner = 2 * x + place
            for h in range(own):
                up_ref[owner * own + h] = ref[x, h * N:(h + 1) * N, :]
            down_ref[pl.ds(pl.multiple_of(owner * rows, 16), rows), :] = ref[x, own * N:own * N + rows, :]
            at = own * N + rows
            betas_ref[owner] = ref[x, at:, :]
            for a in range(0, rows, N):
                size = min(N, rows - a)
                start = pl.multiple_of(owner * rows + a, 16)
                logits += dot(ref[x, at:at + heads, 0:size], turned_ref[pl.ds(start, size), :])
                at += heads
    low_ref[...] = dot(hidden_ref[...], down_ref[...]).astype(BF)
    gate_ref[...] = jax.nn.sigmoid(pad_to_square(logits).T[:, 0:heads])


def first_kernel(low_ref, up_ref, bias_ref, rate_ref, beta_ref, q_ref, k_ref, g_ref,
                 send_ref, inv_ref, mix_ref, sco_ref, cum_ref):
    count = inv_ref.shape[0]
    base = pl.program_id(0) * count
    row, col = iotas()
    tri = ones_where(row >= col)
    cols = head_columns(count)
    each = lambda f: [f(i) for i in range(count)]
    gate = each(lambda i: dot(low_ref[...], up_ref[i]) + bias_ref[:, cols[i]])
    decay = each(lambda i: split3(-rate_ref[:, cols[i]] * softplus(gate[i])))
    cum = each(lambda i: sum(dot(tri, piece) for piece in decay[i]))
    for i in range(count):
        cum_ref[i] = cum[i]
    last = each(lambda i: cum[i][N - 1:N, :])
    qn = each(lambda i: unit(q_ref[:, cols[i]].astype(F32))[0])
    kn = each(lambda i: unit(k_ref[:, cols[i]].astype(F32))[0])
    scale = each(lambda i: jnp.exp(cum[i]))
    kp = each(lambda i: kn[i] * scale[i])
    qp = each(lambda i: qn[i] * scale[i])
    km = each(lambda i: split(kn[i] * jnp.exp(-cum[i])))
    beta = each(lambda i: column(beta_ref[...], base + i))
    mix = each(lambda i: jnp.where(row > col, mm(split(kp[i]), km[i], 1, 1), 0.0))
    sco = each(lambda i: jnp.where(row >= col, mm(split(qp[i]), km[i], 1, 1), 0.0))
    for i in range(count):
        mix_ref[i] = mix[i]
        sco_ref[i] = sco[i]
    inv = inverses(each(lambda i: mix[i] * beta[i]), row, col)
    for i in range(count):
        inv_ref[i] = inv[i]
    z = each(lambda i: split(mm(split(inv[i]), split(kp[i] * beta[i]))))
    seen = each(lambda i: split(qp[i] - mm(split(sco[i]), z[i])))
    local = each(lambda i: mm(seen[i], [g_ref[:, cols[i]]], 0, 0))
    ke = each(lambda i: split(kn[i] * jnp.exp(last[i] - cum[i])))
    moving = each(lambda i: jnp.where(row == col, jnp.exp(last[i]), 0.0) - mm(z[i], ke[i], 0, 0))
    for i in range(count):
        send_ref[i, 0:N, :] = moving[i].astype(BF)
        send_ref[i, N:2 * N, :] = local[i].astype(BF)


def chain_kernel(got_ref, map_ref, sum_ref, tot_ref):
    blocks = got_ref.shape[0]
    run = min(RUN, blocks)
    starts = range(0, blocks, run)
    local = {}
    for a in starts:
        last = a + run - 1
        local[last] = jnp.concatenate(
            [got_ref[last, 0:N, :], got_ref[last, N:2 * N, :]], axis=1).astype(F32)
    for back in range(run - 2, -1, -1):
        for a in starts:
            both = mm([got_ref[a + back, 0:N, :]], split(local[a + back + 1]))
            local[a + back] = jnp.concatenate(
                [both[:, :N], both[:, N:] + got_ref[a + back, N:2 * N, :].astype(F32)], axis=1)

    def after(one, total):
        both = mm(split(one[:, :N]), total)
        return jnp.concatenate([both[:, :N], both[:, N:] + one[:, N:]], axis=1)

    totals = {}
    for a in reversed(starts):
        if a + run < blocks:
            local[a] = after(local[a], totals[a + run])
        totals[a] = split(local[a])
    tot_ref[...] = local[0][:, N:].astype(BF)
    for a in starts:
        for j in range(a, a + run):
            both = local[j] if j == a or a + run == blocks else after(local[j], totals[a + run])
            map_ref[j] = both[:, :N].astype(BF)
            sum_ref[j] = both[:, N:]


def apply_kernel(map_ref, sum_ref, later_ref, end_ref):
    blocks = map_ref.shape[0]
    later = later_ref[...]
    end_ref[blocks - 1] = later
    for j in range(blocks - 1):
        end_ref[j] = (dot(map_ref[j + 1], later) + sum_ref[j + 1]).astype(BF)


def middle_kernel(low_ref, up_ref, bias_ref, rate_ref, beta_ref, q_ref, k_ref, v_ref, g_ref, start_ref, inv_ref, sco_ref, cum_ref,
                  qg_ref, rest_ref, upd_ref, y_ref, kms_ref, term_ref, soft_ref, slope_ref):
    count = inv_ref.shape[0]
    base = pl.program_id(0) * count
    row, col = iotas()
    cols = head_columns(count)
    each = lambda f: [f(i) for i in range(count)]
    cum = each(lambda i: cum_ref[i])
    q = each(lambda i: unit(q_ref[:, cols[i]].astype(F32)))
    kn = each(lambda i: unit(k_ref[:, cols[i]].astype(F32))[0])
    plus = each(lambda i: jnp.exp(cum[i]))
    qp = each(lambda i: q[i][0] * plus[i])
    km = each(lambda i: split(kn[i] * jnp.exp(-cum[i])))
    beta = each(lambda i: column(beta_ref[...], base + i))
    grad = each(lambda i: [g_ref[:, cols[i]]])
    start = each(lambda i: split(start_ref[i]))
    inv = each(lambda i: split(inv_ref[i]))
    rest = each(lambda i: v_ref[:, cols[i]].astype(F32) - mm(split(kn[i] * plus[i]), start[i]))
    upd = each(lambda i: mm(inv[i], split(rest[i] * beta[i])))
    y = each(lambda i: mm(inv[i], split(mm(split(sco_ref[i]), grad[i], 0, 0)), 0, 0))
    upd_s = each(lambda i: split(upd[i]))
    sco_cot = each(lambda i: split(jnp.where(row >= col, mm(grad[i], upd_s[i], 1, 1), 0.0)))
    qp_cot = each(lambda i: mm(grad[i], start[i], 1, 1) + mm(sco_cot[i], km[i]))
    kms = each(lambda i: mm(sco_cot[i], split(qp[i]), 0, 0))
    qn_cot = each(lambda i: qp_cot[i] * plus[i])
    for i in range(count):
        rest_ref[i] = rest[i]
        upd_ref[i] = upd[i]
        y_ref[i] = y[i]
        kms_ref[i] = kms[i]
        term_ref[i] = qp_cot[i] * qp[i]
    gate = each(lambda i: dot(low_ref[...], up_ref[i]) + bias_ref[:, cols[i]])
    for i in range(count):
        soft_ref[i] = softplus(gate[i])
        slope_ref[i] = -rate_ref[:, cols[i]] * jax.nn.sigmoid(gate[i])
        qg_ref[:, cols[i]] = (q[i][1] * (
            qn_cot[i] - q[i][0] * jnp.sum(qn_cot[i] * q[i][0], axis=1, keepdims=True))).astype(BF)


def second_kernel(core_ref, up_ref, beta_ref, k_ref, start_ref, end_ref,
                  inv_ref, mix_ref, cum_ref, rest_ref, upd_ref, y_ref, kms_ref, term_ref,
                  soft_ref, slope_ref, kg_ref, vg_ref, keep_ref, give_ref, lowg_ref, score_ref, low_acc, score_acc, vec_acc):
    count = inv_ref.shape[0]
    step = pl.program_id(0)
    base = step * count
    row, col = iotas()
    upper = ones_where(row <= col)
    ones = jnp.ones((8, N), BF)

    @pl.when(step == 0)
    def _():
        low_acc[...] = jnp.zeros_like(low_acc)
        score_acc[...] = jnp.zeros_like(score_acc)

    cols = head_columns(count)
    each = lambda f: [f(i) for i in range(count)]
    cum = each(lambda i: cum_ref[i])
    last = each(lambda i: cum[i][N - 1:N, :])
    k = each(lambda i: unit(k_ref[:, cols[i]].astype(F32)))
    plus = each(lambda i: jnp.exp(cum[i]))
    minus = each(lambda i: jnp.exp(-cum[i]))
    ending = each(lambda i: jnp.exp(last[i] - cum[i]))
    kp = each(lambda i: k[i][0] * plus[i])
    km = each(lambda i: k[i][0] * minus[i])
    ke = each(lambda i: k[i][0] * ending[i])
    beta = each(lambda i: column(beta_ref[...], base + i))
    end = each(lambda i: [end_ref[i]])
    upd = each(lambda i: split(upd_ref[i]))
    y = each(lambda i: y_ref[i] + mm(split(inv_ref[i]), split(mm(split(ke[i]), end[i])), 0, 0))
    rest_cot = each(lambda i: y[i] * beta[i])
    for i in range(count):
        vg_ref[:, cols[i]] = rest_cot[i].astype(BF)
    outer = each(lambda i: jnp.where(row > col, mm(split(y[i]), upd[i], 1, 1), 0.0))
    beta_cot = each(lambda i: jnp.sum(y[i] * rest_ref[i] - outer[i] * mix_ref[i], axis=1, keepdims=True))
    mix_cot = each(lambda i: split(-outer[i] * beta[i]))
    kp_cot = each(lambda i: mm(mix_cot[i], split(km[i]))
                  - mm(split(rest_cot[i]), split(start_ref[i]), 1, 1))
    km_cot = each(lambda i: mm(mix_cot[i], split(kp[i]), 0, 0) + kms_ref[i])
    ke_cot = each(lambda i: mm(upd[i], end[i], 1, 1))
    last_cot = each(lambda i: jnp.sum(ke_cot[i] * ke[i], axis=0, keepdims=True) + jnp.exp(last[i]) * sum(
        dot(ones, piece, 1, 1) for piece in split3(start_ref[i] * end_ref[i].astype(F32)))[0:1, :])
    cum_cot = each(lambda i: split3(
        term_ref[i] + kp_cot[i] * kp[i] - km_cot[i] * km[i] - ke_cot[i] * ke[i]))
    decay_cot = each(lambda i: sum(dot(upper, piece) for piece in cum_cot[i]) + last_cot[i])
    kn_cot = each(lambda i: kp_cot[i] * plus[i] + km_cot[i] * minus[i] + ke_cot[i] * ending[i])
    for i in range(count):
        kg_ref[:, cols[i]] = (k[i][1] * (
            kn_cot[i] - k[i][0] * jnp.sum(kn_cot[i] * k[i][0], axis=1, keepdims=True))).astype(BF)
    up = each(lambda i: up_ref[i])
    input_grad = each(lambda i: decay_cot[i] * slope_ref[i])
    half = each(lambda i: input_grad[i].astype(BF))
    heads = vec_acc.shape[0] // 2
    even = core_ref[0] == 0
    span = count // 2 * N
    at = pl.multiple_of(step * span, N)
    first, second = (jnp.concatenate(half[a:a + count // 2], axis=0) for a in (0, count // 2))
    keep_ref[pl.ds(at, span), :] = jnp.where(even, first, second)
    give_ref[pl.ds(at, span), :] = jnp.where(even, second, first)
    for i in range(count):
        vec_acc[pl.ds(base + i, 1), :] = jnp.sum(input_grad[i], axis=0, keepdims=True)
        vec_acc[pl.ds(heads + base + i, 1), :] = -jnp.sum(
            decay_cot[i] * soft_ref[i], axis=0, keepdims=True)
    low_acc[...] += sum(each(lambda i: dot(half[i], up[i], 1, 1)))
    score_acc[...] += sum(each(lambda i: jnp.where(
        col == base + i, beta_cot[i] * beta[i] * (1.0 - beta[i]), 0.0)))

    @pl.when(step == pl.num_programs(0) - 1)
    def _():
        low = low_acc[...].astype(BF)
        score = score_acc[...].T[0:score_ref.shape[0], :].astype(BF)
        lowg_ref[...] = low
        score_ref[...] = score
        common = jnp.concatenate([low, score] + split(vec_acc[...]), axis=0)
        keep_ref[heads // 2 * N:, :] = common
        give_ref[heads // 2 * N:, :] = common


def terms_kernel(core_ref, hid_ref, hid2_ref, rank_ref, rank2_ref, keep_ref, got_ref, out_ref, *,
                 own, rows):
    pairs = out_ref.shape[0]
    core = core_ref[0]
    halves = pairs * own * N
    both = lambda a, b: jnp.concatenate(
        [keep_ref[halves + a:halves + b, :], got_ref[halves + a:halves + b, :]], axis=0)
    low = both(0, N)
    score = jnp.concatenate([keep_ref[halves + N:halves + N + 16, :],
                             got_ref[halves + N:halves + N + 16, :]], axis=1)
    at = halves + N + 16
    vec = keep_ref[at:, :].astype(F32) + got_ref[at:, :].astype(F32)
    vec = vec[:vec.shape[0] // 2] + vec[vec.shape[0] // 2:]
    rank = jnp.concatenate([rank_ref[...], rank2_ref[...]], axis=0)
    for x in range(pairs):
        start = pl.multiple_of((2 * x + core) * rows, 16)
        hid = jnp.concatenate([hid_ref[pl.ds(start, rows), :], hid2_ref[pl.ds(start, rows), :]], axis=1)
        parts = []
        for h in range(own):
            a = (x * own + h) * N
            half = jnp.concatenate([keep_ref[a:a + N, :], got_ref[a:a + N, :]], axis=0)
            parts.append(dot(rank, half, 0, 0))
        parts += [dot(hid, low), vec]
        beta = dot(score, hid, 1, 1)
        for a in range(0, rows, N):
            piece = beta[:, a:min(a + N, rows)]
            if piece.shape[1] < N:
                piece = jnp.concatenate([piece, jnp.zeros((16, N - piece.shape[1]), F32)], axis=1)
            parts.append(piece)
        out_ref[x] = jnp.concatenate(parts, axis=0).astype(out_ref.dtype)


def unpack_kernel(sum_ref, down_ref, up_ref, beta_ref, bias_ref, rate_ref):
    heads, rows = beta_ref.shape
    at = 0
    for a in range(0, up_ref.shape[1], N):
        up_ref[:, a:a + N] = sum_ref[at:at + N, :].astype(F32)
        at += N
    down_ref[...] = sum_ref[at:at + rows, :].astype(F32)
    at += rows
    bias_ref[...] = sum_ref[at:at + heads, :].astype(F32)
    rate_ref[...] = sum_ref[at + heads:at + 2 * heads, :].astype(F32)
    at += 2 * heads
    for a in range(0, rows, N):
        size = min(N, rows - a)
        beta_ref[:, a:a + size] = sum_ref[at:at + heads, 0:size].astype(F32)
        at += heads


def call(kernel, name, mib=MIB, **kw):
    return pl.pallas_call(kernel, interpret=INTERPRET, name=name,
                          compiler_params=pltpu.CompilerParams(vmem_limit_bytes=mib << 20), **kw)


def shape(dims, dtype):
    return jax.ShapeDtypeStruct(dims, dtype)


def on_device(nf, ny, nz, hidden, query_heads, key_heads, value_heads, out_grad, checkpoint,
              gate_down, gate_up, gate_bias, decay_rate, beta_weight):
    tok, width = hidden.shape[1], hidden.shape[2]
    heads = checkpoint.shape[2]
    inner = heads * N
    rows = width // nf
    own = heads // nf
    assert ny == 2 and nz == heads
    hidden_rows = hidden.reshape(tok, width)

    up_rows = own * N
    pieces = -(-rows // N)
    weight_rows = up_rows + rows + pieces * heads
    turned = hidden_rows.T
    message = call(pack_kernel, "pack", out_shape=shape((nf // 2, weight_rows, N), BF))(
        gate_up, gate_down, beta_weight.T)
    got = lax.all_to_all(message, "x", 0, 0, tiled=True)
    swapped = lax.ppermute(got, "core", [(0, 1), (1, 0)])
    core = lax.axis_index("core").astype(jnp.int32).reshape(1)
    vmem = pl.BlockSpec(memory_space=pltpu.VMEM)
    ups, down_full, betas, low_rank, beta_gate = call(
        functools.partial(arrange_kernel, rows=rows), "arrange",
        in_specs=[pl.BlockSpec(memory_space=pltpu.SMEM)] + [vmem] * 4,
        out_shape=[shape((heads, N, N), BF), shape((width, N), BF),
                   shape((nf, pieces * heads, N), BF), shape((tok, N), BF), shape((tok, heads), F32)],
    )(core, got, swapped, hidden_rows, turned)
    betas = betas.reshape(nf, pieces, heads, N).transpose(2, 0, 1, 3)
    betas = betas.reshape(heads, nf, pieces * N)[:, :, :rows].reshape(heads, width)
    bias = gate_bias.reshape(1, inner)
    rate = decay_rate.reshape(1, inner)
    q, k, v, g = (x.reshape(tok, inner) for x in (query_heads, key_heads, value_heads, out_grad))
    start = checkpoint.reshape(heads, N, N)

    whole = lambda dims: pl.BlockSpec(dims, lambda i: (0,) * len(dims))
    row_spec = lambda hb: pl.BlockSpec((1, hb * N), lambda i: (0, i))
    tok_spec = lambda hb: pl.BlockSpec((N, hb * N), lambda i: (0, i))
    mat_spec = lambda hb: pl.BlockSpec((hb, N, N), lambda i: (i, 0, 0))
    gate_specs = lambda hb: [
        whole((tok, N)), mat_spec(hb), row_spec(hb), row_spec(hb), whole((tok, heads))]
    gate_args = (low_rank, ups, bias, rate, beta_gate)
    mat = shape((heads, N, N), F32)
    cost = pl.CostEstimate(flops=4 * 10**9, bytes_accessed=12 << 20, transcendentals=0)

    hb = FIRST_HB
    send, inv, mix, sco, cum = call(
        first_kernel, "first", 28,
        grid=(heads // hb,),
        in_specs=gate_specs(hb) + [tok_spec(hb)] * 3,
        out_specs=[pl.BlockSpec((hb, 2 * N, N), lambda i: (i, 0, 0))] + [mat_spec(hb)] * 4,
        out_shape=[shape((heads, 2 * N, N), BF)] + [mat] * 4,
    )(*gate_args, q, k, g)

    spread = lax.all_to_all(send, "z", 0, 0, tiled=True)

    hb = HB
    q_grad, rest, upd, y, kms, term, soft, slope = call(
        middle_kernel, "middle", 56,
        grid=(heads // hb,),
        in_specs=gate_specs(hb) + [tok_spec(hb)] * 4 + [mat_spec(hb)] * 4,
        out_specs=[tok_spec(hb)] + [mat_spec(hb)] * 7,
        out_shape=[shape((tok, inner), BF)] + [mat] * 7,
        cost_estimate=cost,
    )(*gate_args, q, k, v, g, start, inv, sco, cum)

    maps, adds, total = call(
        chain_kernel, "chain",
        out_shape=[shape((heads, N, N), BF), mat, shape((N, N), BF)],
    )(spread)
    later = lax.ppermute(total, "y", [(1, 0)])
    end = call(apply_kernel, "apply", out_shape=shape((heads, N, N), BF))(maps, adds, later)
    end = lax.all_to_all(end, "z", 0, 0, tiled=True)

    swap = [(0, 1), (1, 0)]
    turned2 = lax.ppermute(turned, "core", swap)
    low_rank2 = lax.ppermute(low_rank, "core", swap)

    assert hb == 2 * own
    keep_rows = heads // 2 * N + N + heads + 4 * heads
    k_grad, v_grad, keep, give, low_grad, score = call(
        second_kernel, "second", 56,
        grid=(heads // hb,),
        in_specs=[pl.BlockSpec(memory_space=pltpu.SMEM), mat_spec(hb), whole((tok, heads)), tok_spec(hb)] + [mat_spec(hb)] * 12,
        out_specs=[tok_spec(hb)] * 2 + [whole((keep_rows, N))] * 2 + [whole((N, N)), whole((heads, N))],
        out_shape=[shape((tok, inner), BF)] * 2 + [shape((keep_rows, N), BF)] * 2 + [
            shape((N, N), BF), shape((heads, N), BF)],
        scratch_shapes=[pltpu.VMEM((N, N), F32)] * 2 + [pltpu.VMEM((2 * heads, N), F32)],
        cost_estimate=cost,
    )(core, ups, beta_gate, k, start, end, inv, mix, cum, rest, upd, y, kms, term, soft, slope)

    given = lax.ppermute(give, "core", swap)
    used = own * N + rows + 2 * heads + pieces * heads
    terms = call(
        functools.partial(terms_kernel, own=own, rows=rows), "terms",
        in_specs=[pl.BlockSpec(memory_space=pltpu.SMEM)] + [vmem] * 6,
        out_shape=shape((nf // 2, used, N), LINK),
    )(core, turned, turned2, low_rank, low_rank2, keep, given)
    terms = lax.all_to_all(terms, "x", 0, 0, tiled=True)
    parts = ny * nz
    chunk = 8 * -(-used // (8 * parts))
    sums = jnp.sum(terms.astype(F32), axis=0).astype(LINK)
    sums = jnp.pad(sums, ((0, parts * chunk - used), (0, 0))).reshape(parts, chunk, N)
    sums = lax.all_to_all(sums, ("y", "z"), 0, 0, tiled=True)
    sums = jnp.sum(sums.astype(F32), axis=0).astype(LINK)
    sums = lax.all_to_all(jnp.broadcast_to(sums[None], (parts, chunk, N)), ("y", "z"), 0, 0, tiled=True)
    down_grad, up_grad, beta_grad, bias_grad, rate_grad = call(
        unpack_kernel, "unpack",
        out_shape=[shape((rows, N), F32), shape((N, own * N), F32), shape((heads, rows), F32),
                   shape((heads, N), F32), shape((heads, N), F32)],
    )(sums.reshape(parts * chunk, N))

    hidden_grad = (
        lax.dot_general(low_grad, down_full, (((1,), (1,)), ((), ())), preferred_element_type=F32)
        + lax.dot_general(score, betas, (((0,), (0,)), ((), ())), preferred_element_type=F32)
    ).astype(BF)

    return (q_grad[None], k_grad[None], v_grad[None], hidden_grad[None],
            down_grad, up_grad, beta_grad.T, bias_grad.reshape(inner), rate_grad.reshape(inner))


def grid_of(size, heads=16):
    return size // heads, heads


def solution(mesh):
    nf, size = mesh.shape["fsdp"], mesh.shape["ctx"]
    ny, nz = grid_of(size)
    fine = Mesh(mesh.devices.reshape(nf // 2, 2, ny, nz), ("x", "core", "y", "z"))
    fsdp, ctx = ("x", "core"), ("y", "z")
    tokens = P(fsdp, ctx, None)
    return jax.shard_map(
        functools.partial(on_device, nf, ny, nz),
        mesh=fine,
        in_specs=(tokens,) * 5 + (
            P(fsdp, ctx, None, None, None), P(fsdp, None), P(None, fsdp), P(), P(),
            P(fsdp, None)),
        out_specs=(tokens,) * 4 + (
            P(fsdp, None), P(None, fsdp), P(fsdp, None), P(), P()),
        check_vma=False,
    )
```

```python
import functools

import jax
import jax.numpy as jnp
from jax import lax
from jax.experimental import pallas as pl
from jax.experimental.pallas import tpu as pltpu
from jax.sharding import Mesh, PartitionSpec as P

EPSILON = 1e-06
BF = jnp.bfloat16
F32 = jnp.float32
N = 128
HB = 4
FIRST_HB = 16
LINK = jnp.bfloat16
RUN = 4
MIB = 28
INTERPRET = False


def split(x):
    hi = x.astype(BF)
    return [hi, (x - hi.astype(F32)).astype(BF)]


def split3(x):
    hi = x.astype(BF)
    rest = x - hi.astype(F32)
    mid = rest.astype(BF)
    return [hi, mid, (rest - mid.astype(F32)).astype(BF)]


def dot(a, b, ca=1, cb=0):
    return lax.dot_general(a, b, (((ca,), (cb,)), ((), ())), preferred_element_type=F32)


def mm(a, b, ca=1, cb=0):
    if len(a) > 1 and len(b) > 1:
        both = jnp.concatenate(b, axis=1 - cb)
        both = dot(jnp.concatenate(a, axis=ca), jnp.concatenate([both, both], axis=cb), ca, cb)
        half = both.shape[1] // 2
        return both[:, :half] + both[:, half:]
    if len(a) > 1:
        return dot(jnp.concatenate(a, axis=ca), jnp.concatenate([b[0], b[0]], axis=cb), ca, cb)
    return sum(dot(a[0], part, ca, cb) for part in b)


def iotas():
    return lax.broadcasted_iota(jnp.int32, (N, N), 0), lax.broadcasted_iota(jnp.int32, (N, N), 1)


def ones_where(cond):
    return jnp.where(cond, 1.0, 0.0).astype(BF)


def softplus(x):
    return jnp.maximum(x, 0.0) + jnp.log1p(jnp.exp(-jnp.abs(x)))


def unit(x):
    scale = lax.rsqrt(jnp.sum(x * x, axis=-1, keepdims=True) + EPSILON)
    return x * scale, scale


def column(values, index):
    lane = lax.broadcasted_iota(jnp.int32, values.shape, 1)
    return jnp.sum(jnp.where(lane == index, values, 0.0), axis=1, keepdims=True)


def inverses(stricts, row, col):
    near = (row >> 3) == (col >> 3)
    gather = ones_where(near)
    lane = lax.broadcasted_iota(jnp.int32, (8, N), 1) & 7
    sub = lax.broadcasted_iota(jnp.int32, (8, N), 0)
    invs = []
    for strict in stricts:
        block = jnp.where(near, strict, 0.0)
        block = sum(block[8 * i:8 * i + 8] for i in range(N // 8))
        picked = split3(jnp.concatenate([jnp.where(lane == k, block, 0.0) for k in range(8)], axis=0))
        spread = sum(dot(part, gather) for part in picked)
        inv = jnp.where(lane == sub, 1.0, 0.0)
        for k in range(7):
            inv = inv - spread[8 * k:8 * k + 8] * inv[k:k + 1, :]
        invs.append(jnp.where(near, jnp.concatenate([inv] * (N // 8), axis=0), 0.0))
    for bit in range(3, 7):
        pick = ((row >> (bit + 1)) == (col >> (bit + 1))) & ((row >> bit) != (col >> bit))
        parts = [split(inv) for inv in invs]
        offs = [split(jnp.where(pick, strict, 0.0)) for strict in stricts]
        offs = [split(mm(part, off)) for part, off in zip(parts, offs)]
        invs = [inv - mm(off, part) for inv, off, part in zip(invs, offs, parts)]
    return invs


def head_columns(count):
    return [slice(i * N, (i + 1) * N) for i in range(count)]


def pad_to_square(x):
    if x.shape[0] < N:
        x = jnp.concatenate([x, jnp.zeros((N - x.shape[0], x.shape[1]), x.dtype)], axis=0)
    if x.shape[1] < N:
        x = jnp.concatenate([x, jnp.zeros((N, N - x.shape[1]), x.dtype)], axis=1)
    return x


def widen(x):
    if x.shape[1] == N:
        return x
    return jnp.concatenate([x, jnp.zeros((x.shape[0], N - x.shape[1]), x.dtype)], axis=1)


def pack_kernel(up_ref, down_ref, beta_ref, out_ref):
    rows = beta_ref.shape[1]
    parts = [up_ref[:, a:a + N] for a in range(0, up_ref.shape[1], N)] + [down_ref[...]]
    parts += [widen(beta_ref[:, a:min(a + N, rows)]) for a in range(0, rows, N)]
    mine = jnp.concatenate(parts, axis=0)
    for r in range(out_ref.shape[0]):
        out_ref[r] = mine


def arrange_kernel(core_ref, ours_ref, theirs_ref, hidden_ref, turned_ref,
                   up_ref, down_ref, betas_ref, low_ref, gate_ref, *, rows):
    pairs = ours_ref.shape[0]
    heads = gate_ref.shape[1]
    own = up_ref.shape[0] // (2 * pairs)
    core = core_ref[0]
    logits = jnp.zeros((heads, N), F32)
    for ref, place in ((ours_ref, core), (theirs_ref, 1 - core)):
        for x in range(pairs):
            owner = 2 * x + place
            for h in range(own):
                up_ref[owner * own + h] = ref[x, h * N:(h + 1) * N, :]
            down_ref[pl.ds(pl.multiple_of(owner * rows, 16), rows), :] = ref[x, own * N:own * N + rows, :]
            at = own * N + rows
            betas_ref[owner] = ref[x, at:, :]
            for a in range(0, rows, N):
                size = min(N, rows - a)
                start = pl.multiple_of(owner * rows + a, 16)
                logits += dot(ref[x, at:at + heads, 0:size], turned_ref[pl.ds(start, size), :])
                at += heads
    low_ref[...] = dot(hidden_ref[...], down_ref[...]).astype(BF)
    gate_ref[...] = jax.nn.sigmoid(pad_to_square(logits).T[:, 0:heads])


def first_kernel(low_ref, up_ref, bias_ref, rate_ref, beta_ref, q_ref, k_ref, g_ref,
                 send_ref, inv_ref, mix_ref, sco_ref, cum_ref):
    count = inv_ref.shape[0]
    base = pl.program_id(0) * count
    row, col = iotas()
    tri = ones_where(row >= col)
    cols = head_columns(count)
    each = lambda f: [f(i) for i in range(count)]
    gate = each(lambda i: dot(low_ref[...], up_ref[i]) + bias_ref[:, cols[i]])
    decay = each(lambda i: split3(-rate_ref[:, cols[i]] * softplus(gate[i])))
    cum = each(lambda i: sum(dot(tri, piece) for piece in decay[i]))
    for i in range(count):
        cum_ref[i] = cum[i]
    last = each(lambda i: cum[i][N - 1:N, :])
    qn = each(lambda i: unit(q_ref[:, cols[i]].astype(F32))[0])
    kn = each(lambda i: unit(k_ref[:, cols[i]].astype(F32))[0])
    scale = each(lambda i: jnp.exp(cum[i]))
    kp = each(lambda i: kn[i] * scale[i])
    qp = each(lambda i: qn[i] * scale[i])
    km = each(lambda i: split(kn[i] * jnp.exp(-cum[i])))
    beta = each(lambda i: column(beta_ref[...], base + i))
    mix = each(lambda i: jnp.where(row > col, mm(split(kp[i]), km[i], 1, 1), 0.0))
    sco = each(lambda i: jnp.where(row >= col, mm(split(qp[i]), km[i], 1, 1), 0.0))
    for i in range(count):
        mix_ref[i] = mix[i]
        sco_ref[i] = sco[i]
    inv = inverses(each(lambda i: mix[i] * beta[i]), row, col)
    for i in range(count):
        inv_ref[i] = inv[i]
    z = each(lambda i: split(mm(split(inv[i]), split(kp[i] * beta[i]))))
    seen = each(lambda i: split(qp[i] - mm(split(sco[i]), z[i])))
    local = each(lambda i: mm(seen[i], [g_ref[:, cols[i]]], 0, 0))
    ke = each(lambda i: split(kn[i] * jnp.exp(last[i] - cum[i])))
    moving = each(lambda i: jnp.where(row == col, jnp.exp(last[i]), 0.0) - mm(z[i], ke[i], 0, 0))
    for i in range(count):
        send_ref[i, 0:N, :] = moving[i].astype(BF)
        send_ref[i, N:2 * N, :] = local[i].astype(BF)


def chain_kernel(got_ref, map_ref, sum_ref, tot_ref):
    blocks = got_ref.shape[0]
    run = min(RUN, blocks)
    starts = range(0, blocks, run)
    local = {}
    for a in starts:
        last = a + run - 1
        local[last] = jnp.concatenate(
            [got_ref[last, 0:N, :], got_ref[last, N:2 * N, :]], axis=1).astype(F32)
    for back in range(run - 2, -1, -1):
        for a in starts:
            both = mm([got_ref[a + back, 0:N, :]], split(local[a + back + 1]))
            local[a + back] = jnp.concatenate(
                [both[:, :N], both[:, N:] + got_ref[a + back, N:2 * N, :].astype(F32)], axis=1)

    def after(one, total):
        both = mm(split(one[:, :N]), total)
        return jnp.concatenate([both[:, :N], both[:, N:] + one[:, N:]], axis=1)

    totals = {}
    for a in reversed(starts):
        if a + run < blocks:
            local[a] = after(local[a], totals[a + run])
        totals[a] = split(local[a])
    tot_ref[...] = local[0][:, N:].astype(BF)
    for a in starts:
        for j in range(a, a + run):
            both = local[j] if j == a or a + run == blocks else after(local[j], totals[a + run])
            map_ref[j] = both[:, :N].astype(BF)
            sum_ref[j] = both[:, N:]


def apply_kernel(map_ref, sum_ref, later_ref, end_ref):
    blocks = map_ref.shape[0]
    later = later_ref[...]
    end_ref[blocks - 1] = later
    for j in range(blocks - 1):
        end_ref[j] = (dot(map_ref[j + 1], later) + sum_ref[j + 1]).astype(BF)


def middle_kernel(low_ref, up_ref, bias_ref, rate_ref, beta_ref, q_ref, k_ref, v_ref, g_ref, start_ref, inv_ref, sco_ref, cum_ref,
                  qg_ref, rest_ref, upd_ref, y_ref, kms_ref, term_ref, soft_ref, slope_ref):
    count = inv_ref.shape[0]
    base = pl.program_id(0) * count
    row, col = iotas()
    cols = head_columns(count)
    each = lambda f: [f(i) for i in range(count)]
    cum = each(lambda i: cum_ref[i])
    q = each(lambda i: unit(q_ref[:, cols[i]].astype(F32)))
    kn = each(lambda i: unit(k_ref[:, cols[i]].astype(F32))[0])
    plus = each(lambda i: jnp.exp(cum[i]))
    qp = each(lambda i: q[i][0] * plus[i])
    km = each(lambda i: split(kn[i] * jnp.exp(-cum[i])))
    beta = each(lambda i: column(beta_ref[...], base + i))
    grad = each(lambda i: [g_ref[:, cols[i]]])
    start = each(lambda i: split(start_ref[i]))
    inv = each(lambda i: split(inv_ref[i]))
    rest = each(lambda i: v_ref[:, cols[i]].astype(F32) - mm(split(kn[i] * plus[i]), start[i]))
    upd = each(lambda i: mm(inv[i], split(rest[i] * beta[i])))
    y = each(lambda i: mm(inv[i], split(mm(split(sco_ref[i]), grad[i], 0, 0)), 0, 0))
    upd_s = each(lambda i: split(upd[i]))
    sco_cot = each(lambda i: split(jnp.where(row >= col, mm(grad[i], upd_s[i], 1, 1), 0.0)))
    qp_cot = each(lambda i: mm(grad[i], start[i], 1, 1) + mm(sco_cot[i], km[i]))
    kms = each(lambda i: mm(sco_cot[i], split(qp[i]), 0, 0))
    qn_cot = each(lambda i: qp_cot[i] * plus[i])
    for i in range(count):
        rest_ref[i] = rest[i]
        upd_ref[i] = upd[i]
        y_ref[i] = y[i]
        kms_ref[i] = kms[i]
        term_ref[i] = qp_cot[i] * qp[i]
    gate = each(lambda i: dot(low_ref[...], up_ref[i]) + bias_ref[:, cols[i]])
    for i in range(count):
        soft_ref[i] = softplus(gate[i])
        slope_ref[i] = -rate_ref[:, cols[i]] * jax.nn.sigmoid(gate[i])
        qg_ref[:, cols[i]] = (q[i][1] * (
            qn_cot[i] - q[i][0] * jnp.sum(qn_cot[i] * q[i][0], axis=1, keepdims=True))).astype(BF)


def second_kernel(core_ref, up_ref, beta_ref, k_ref, start_ref, end_ref,
                  inv_ref, mix_ref, cum_ref, rest_ref, upd_ref, y_ref, kms_ref, term_ref,
                  soft_ref, slope_ref, kg_ref, vg_ref, keep_ref, give_ref, lowg_ref, score_ref, low_acc, score_acc, vec_acc):
    count = inv_ref.shape[0]
    step = pl.program_id(0)
    base = step * count
    row, col = iotas()
    upper = ones_where(row <= col)
    ones = jnp.ones((8, N), BF)

    @pl.when(step == 0)
    def _():
        low_acc[...] = jnp.zeros_like(low_acc)
        score_acc[...] = jnp.zeros_like(score_acc)

    cols = head_columns(count)
    each = lambda f: [f(i) for i in range(count)]
    cum = each(lambda i: cum_ref[i])
    last = each(lambda i: cum[i][N - 1:N, :])
    k = each(lambda i: unit(k_ref[:, cols[i]].astype(F32)))
    plus = each(lambda i: jnp.exp(cum[i]))
    minus = each(lambda i: jnp.exp(-cum[i]))
    ending = each(lambda i: jnp.exp(last[i] - cum[i]))
    kp = each(lambda i: k[i][0] * plus[i])
    km = each(lambda i: k[i][0] * minus[i])
    ke = each(lambda i: k[i][0] * ending[i])
    beta = each(lambda i: column(beta_ref[...], base + i))
    end = each(lambda i: [end_ref[i]])
    upd = each(lambda i: split(upd_ref[i]))
    y = each(lambda i: y_ref[i] + mm(split(inv_ref[i]), split(mm(split(ke[i]), end[i])), 0, 0))
    rest_cot = each(lambda i: y[i] * beta[i])
    for i in range(count):
        vg_ref[:, cols[i]] = rest_cot[i].astype(BF)
    outer = each(lambda i: jnp.where(row > col, mm(split(y[i]), upd[i], 1, 1), 0.0))
    beta_cot = each(lambda i: jnp.sum(y[i] * rest_ref[i] - outer[i] * mix_ref[i], axis=1, keepdims=True))
    mix_cot = each(lambda i: split(-outer[i] * beta[i]))
    kp_cot = each(lambda i: mm(mix_cot[i], split(km[i]))
                  - mm(split(rest_cot[i]), split(start_ref[i]), 1, 1))
    km_cot = each(lambda i: mm(mix_cot[i], split(kp[i]), 0, 0) + kms_ref[i])
    ke_cot = each(lambda i: mm(upd[i], end[i], 1, 1))
    last_cot = each(lambda i: jnp.sum(ke_cot[i] * ke[i], axis=0, keepdims=True) + jnp.exp(last[i]) * sum(
        dot(ones, piece, 1, 1) for piece in split3(start_ref[i] * end_ref[i].astype(F32)))[0:1, :])
    cum_cot = each(lambda i: split3(
        term_ref[i] + kp_cot[i] * kp[i] - km_cot[i] * km[i] - ke_cot[i] * ke[i]))
    decay_cot = each(lambda i: sum(dot(upper, piece) for piece in cum_cot[i]) + last_cot[i])
    kn_cot = each(lambda i: kp_cot[i] * plus[i] + km_cot[i] * minus[i] + ke_cot[i] * ending[i])
    for i in range(count):
        kg_ref[:, cols[i]] = (k[i][1] * (
            kn_cot[i] - k[i][0] * jnp.sum(kn_cot[i] * k[i][0], axis=1, keepdims=True))).astype(BF)
    up = each(lambda i: up_ref[i])
    input_grad = each(lambda i: decay_cot[i] * slope_ref[i])
    half = each(lambda i: input_grad[i].astype(BF))
    heads = vec_acc.shape[0] // 2
    even = core_ref[0] == 0
    span = count // 2 * N
    at = pl.multiple_of(step * span, N)
    first, second = (jnp.concatenate(half[a:a + count // 2], axis=0) for a in (0, count // 2))
    keep_ref[pl.ds(at, span), :] = jnp.where(even, first, second)
    give_ref[pl.ds(at, span), :] = jnp.where(even, second, first)
    for i in range(count):
        vec_acc[pl.ds(base + i, 1), :] = jnp.sum(input_grad[i], axis=0, keepdims=True)
        vec_acc[pl.ds(heads + base + i, 1), :] = -jnp.sum(
            decay_cot[i] * soft_ref[i], axis=0, keepdims=True)
    low_acc[...] += sum(each(lambda i: dot(half[i], up[i], 1, 1)))
    score_acc[...] += sum(each(lambda i: jnp.where(
        col == base + i, beta_cot[i] * beta[i] * (1.0 - beta[i]), 0.0)))

    @pl.when(step == pl.num_programs(0) - 1)
    def _():
        low = low_acc[...].astype(BF)
        score = score_acc[...].T[0:score_ref.shape[0], :].astype(BF)
        lowg_ref[...] = low
        score_ref[...] = score
        common = jnp.concatenate([low, score] + split(vec_acc[...]), axis=0)
        keep_ref[heads // 2 * N:, :] = common
        give_ref[heads // 2 * N:, :] = common


def terms_kernel(core_ref, hid_ref, hid2_ref, rank_ref, rank2_ref, keep_ref, got_ref, out_ref, *,
                 own, rows):
    pairs = out_ref.shape[0]
    core = core_ref[0]
    halves = pairs * own * N
    both = lambda a, b: jnp.concatenate(
        [keep_ref[halves + a:halves + b, :], got_ref[halves + a:halves + b, :]], axis=0)
    low = both(0, N)
    score = jnp.concatenate([keep_ref[halves + N:halves + N + 16, :],
                             got_ref[halves + N:halves + N + 16, :]], axis=1)
    at = halves + N + 16
    vec = keep_ref[at:, :].astype(F32) + got_ref[at:, :].astype(F32)
    vec = vec[:vec.shape[0] // 2] + vec[vec.shape[0] // 2:]
    rank = jnp.concatenate([rank_ref[...], rank2_ref[...]], axis=0)
    for x in range(pairs):
        start = pl.multiple_of((2 * x + core) * rows, 16)
        hid = jnp.concatenate([hid_ref[pl.ds(start, rows), :], hid2_ref[pl.ds(start, rows), :]], axis=1)
        parts = []
        for h in range(own):
            a = (x * own + h) * N
            half = jnp.concatenate([keep_ref[a:a + N, :], got_ref[a:a + N, :]], axis=0)
            parts.append(dot(rank, half, 0, 0))
        parts += [dot(hid, low), vec]
        beta = dot(score, hid, 1, 1)
        for a in range(0, rows, N):
            piece = beta[:, a:min(a + N, rows)]
            if piece.shape[1] < N:
                piece = jnp.concatenate([piece, jnp.zeros((16, N - piece.shape[1]), F32)], axis=1)
            parts.append(piece)
        out_ref[x] = jnp.concatenate(parts, axis=0).astype(out_ref.dtype)


def total(ref):
    return sum(ref[r].astype(F32) for r in range(ref.shape[0]))


def total_kernel(in_ref, out_ref):
    rows = in_ref.shape[1]
    out_ref[0:rows, :] = total(in_ref).astype(out_ref.dtype)
    out_ref[rows:, :] = jnp.zeros((out_ref.shape[0] - rows, N), out_ref.dtype)


def share_kernel(in_ref, out_ref):
    mine = total(in_ref).astype(out_ref.dtype)
    for r in range(out_ref.shape[0]):
        out_ref[r] = mine


def unpack_kernel(sum_ref, down_ref, up_ref, beta_ref, bias_ref, rate_ref):
    heads, rows = beta_ref.shape
    at = 0
    for a in range(0, up_ref.shape[1], N):
        up_ref[:, a:a + N] = sum_ref[at:at + N, :].astype(F32)
        at += N
    down_ref[...] = sum_ref[at:at + rows, :].astype(F32)
    at += rows
    bias_ref[...] = sum_ref[at:at + heads, :].astype(F32)
    rate_ref[...] = sum_ref[at + heads:at + 2 * heads, :].astype(F32)
    at += 2 * heads
    for a in range(0, rows, N):
        size = min(N, rows - a)
        beta_ref[:, a:a + size] = sum_ref[at:at + heads, 0:size].astype(F32)
        at += heads


def call(kernel, name, mib=MIB, **kw):
    return pl.pallas_call(kernel, interpret=INTERPRET, name=name,
                          compiler_params=pltpu.CompilerParams(vmem_limit_bytes=mib << 20), **kw)


def shape(dims, dtype):
    return jax.ShapeDtypeStruct(dims, dtype)


def on_device(nf, ny, nz, hidden, query_heads, key_heads, value_heads, out_grad, checkpoint,
              gate_down, gate_up, gate_bias, decay_rate, beta_weight):
    tok, width = hidden.shape[1], hidden.shape[2]
    heads = checkpoint.shape[2]
    inner = heads * N
    rows = width // nf
    own = heads // nf
    assert ny == 2 and nz == heads
    hidden_rows = hidden.reshape(tok, width)

    up_rows = own * N
    pieces = -(-rows // N)
    weight_rows = up_rows + rows + pieces * heads
    turned = hidden_rows.T
    message = call(pack_kernel, "pack", 56, out_shape=shape((nf // 2, weight_rows, N), BF))(
        gate_up, gate_down, beta_weight.T)
    got = lax.all_to_all(message, "x", 0, 0, tiled=True)
    swapped = lax.ppermute(got, "core", [(0, 1), (1, 0)])
    core = lax.axis_index("core").astype(jnp.int32).reshape(1)
    vmem = pl.BlockSpec(memory_space=pltpu.VMEM)
    ups, down_full, betas, low_rank, beta_gate = call(
        functools.partial(arrange_kernel, rows=rows), "arrange",
        in_specs=[pl.BlockSpec(memory_space=pltpu.SMEM)] + [vmem] * 4,
        out_shape=[shape((heads, N, N), BF), shape((width, N), BF),
                   shape((nf, pieces * heads, N), BF), shape((tok, N), BF), shape((tok, heads), F32)],
    )(core, got, swapped, hidden_rows, turned)
    betas = betas.reshape(nf, pieces, heads, N).transpose(2, 0, 1, 3)
    betas = betas.reshape(heads, nf, pieces * N)[:, :, :rows].reshape(heads, width)
    bias = gate_bias.reshape(1, inner)
    rate = decay_rate.reshape(1, inner)
    q, k, v, g = (x.reshape(tok, inner) for x in (query_heads, key_heads, value_heads, out_grad))
    start = checkpoint.reshape(heads, N, N)

    whole = lambda dims: pl.BlockSpec(dims, lambda i: (0,) * len(dims))
    row_spec = lambda hb: pl.BlockSpec((1, hb * N), lambda i: (0, i))
    tok_spec = lambda hb: pl.BlockSpec((N, hb * N), lambda i: (0, i))
    mat_spec = lambda hb: pl.BlockSpec((hb, N, N), lambda i: (i, 0, 0))
    gate_specs = lambda hb: [
        whole((tok, N)), mat_spec(hb), row_spec(hb), row_spec(hb), whole((tok, heads))]
    gate_args = (low_rank, ups, bias, rate, beta_gate)
    mat = shape((heads, N, N), F32)
    cost = pl.CostEstimate(flops=4 * 10**9, bytes_accessed=12 << 20, transcendentals=0)

    hb = FIRST_HB
    send, inv, mix, sco, cum = call(
        first_kernel, "first", 28,
        grid=(heads // hb,),
        in_specs=gate_specs(hb) + [tok_spec(hb)] * 3,
        out_specs=[pl.BlockSpec((hb, 2 * N, N), lambda i: (i, 0, 0))] + [mat_spec(hb)] * 4,
        out_shape=[shape((heads, 2 * N, N), BF)] + [mat] * 4,
    )(*gate_args, q, k, g)

    spread = lax.all_to_all(send, "z", 0, 0, tiled=True)

    hb = HB
    q_grad, rest, upd, y, kms, term, soft, slope = call(
        middle_kernel, "middle", 56,
        grid=(heads // hb,),
        in_specs=gate_specs(hb) + [tok_spec(hb)] * 4 + [mat_spec(hb)] * 4,
        out_specs=[tok_spec(hb)] + [mat_spec(hb)] * 7,
        out_shape=[shape((tok, inner), BF)] + [mat] * 7,
        cost_estimate=cost,
    )(*gate_args, q, k, v, g, start, inv, sco, cum)

    maps, adds, total = call(
        chain_kernel, "chain",
        out_shape=[shape((heads, N, N), BF), mat, shape((N, N), BF)],
    )(spread)
    later = lax.ppermute(total, "y", [(1, 0)])
    end = call(apply_kernel, "apply", out_shape=shape((heads, N, N), BF))(maps, adds, later)
    end = lax.all_to_all(end, "z", 0, 0, tiled=True)

    swap = [(0, 1), (1, 0)]
    turned2 = lax.ppermute(turned, "core", swap)
    low_rank2 = lax.ppermute(low_rank, "core", swap)

    assert hb == 2 * own
    keep_rows = heads // 2 * N + N + heads + 4 * heads
    k_grad, v_grad, keep, give, low_grad, score = call(
        second_kernel, "second", 56,
        grid=(heads // hb,),
        in_specs=[pl.BlockSpec(memory_space=pltpu.SMEM), mat_spec(hb), whole((tok, heads)), tok_spec(hb)] + [mat_spec(hb)] * 12,
        out_specs=[tok_spec(hb)] * 2 + [whole((keep_rows, N))] * 2 + [whole((N, N)), whole((heads, N))],
        out_shape=[shape((tok, inner), BF)] * 2 + [shape((keep_rows, N), BF)] * 2 + [
            shape((N, N), BF), shape((heads, N), BF)],
        scratch_shapes=[pltpu.VMEM((N, N), F32)] * 2 + [pltpu.VMEM((2 * heads, N), F32)],
        cost_estimate=cost,
    )(core, ups, beta_gate, k, start, end, inv, mix, cum, rest, upd, y, kms, term, soft, slope)

    given = lax.ppermute(give, "core", swap)
    used = own * N + rows + 2 * heads + pieces * heads
    terms = call(
        functools.partial(terms_kernel, own=own, rows=rows), "terms",
        in_specs=[pl.BlockSpec(memory_space=pltpu.SMEM)] + [vmem] * 6,
        out_shape=shape((nf // 2, used, N), LINK),
    )(core, turned, turned2, low_rank, low_rank2, keep, given)
    terms = lax.all_to_all(terms, "x", 0, 0, tiled=True)
    parts = ny * nz
    chunk = 8 * -(-used // (8 * parts))
    sums = call(total_kernel, "total", out_shape=shape((parts * chunk, N), LINK))(terms)
    sums = lax.all_to_all(sums.reshape(parts, chunk, N), ("y", "z"), 0, 0, tiled=True)
    sums = call(share_kernel, "share", out_shape=shape((parts, chunk, N), LINK))(sums)
    sums = lax.all_to_all(sums, ("y", "z"), 0, 0, tiled=True)
    down_grad, up_grad, beta_grad, bias_grad, rate_grad = call(
        unpack_kernel, "unpack",
        out_shape=[shape((rows, N), F32), shape((N, own * N), F32), shape((heads, rows), F32),
                   shape((heads, N), F32), shape((heads, N), F32)],
    )(sums.reshape(parts * chunk, N))

    hidden_grad = (
        lax.dot_general(low_grad, down_full, (((1,), (1,)), ((), ())), preferred_element_type=F32)
        + lax.dot_general(score, betas, (((0,), (0,)), ((), ())), preferred_element_type=F32)
    ).astype(BF)

    return (q_grad[None], k_grad[None], v_grad[None], hidden_grad[None],
            down_grad, up_grad, beta_grad.T, bias_grad.reshape(inner), rate_grad.reshape(inner))


def grid_of(size, heads=16):
    return size // heads, heads


def solution(mesh):
    nf, size = mesh.shape["fsdp"], mesh.shape["ctx"]
    ny, nz = grid_of(size)
    fine = Mesh(mesh.devices.reshape(nf // 2, 2, ny, nz), ("x", "core", "y", "z"))
    fsdp, ctx = ("x", "core"), ("y", "z")
    tokens = P(fsdp, ctx, None)
    return jax.shard_map(
        functools.partial(on_device, nf, ny, nz),
        mesh=fine,
        in_specs=(tokens,) * 5 + (
            P(fsdp, ctx, None, None, None), P(fsdp, None), P(None, fsdp), P(), P(),
            P(fsdp, None)),
        out_specs=(tokens,) * 4 + (
            P(fsdp, None), P(None, fsdp), P(fsdp, None), P(), P()),
        check_vma=False,
    )
```
